32 devices in a mesh: paths: 2 (over y), tm: 16 (over z, x, core).
Axes of the slice: x: 2, y: 2, z: 4, core: 2. Of those that a mesh axis runs over, the one named last changes fastest.
Arguments:
- independent_disturbances: bfloat16 [1024, 8, 1024], P('tm', 'paths'), may hold values from -6 to 6
- starting_driver_values: float32 [8, 1024], P('paths'), may hold values from -6 to 6
- correlation_mixer: bfloat16 [1024, 1024], P('paths'), may hold values from -0.1875 to 0.1875
- log_persistence: float32 [1024], replicated, may hold values from -0.034 to 0
- regime_multiplier: float32 [1024], P('tm'), may hold values from 0.5 to 1
- payoff_per_unit_table: bfloat16 [1024, 128], replicated, may hold values from -0.1875 to 0.1875
- short_yield_coefficients: bfloat16 [1024], replicated, may hold values from -0.1875 to 0.1875
Outputs:
- values: float32 [8, 128], P('paths')
The draws below stay inside these ranges and needn't reach their ends.
All inputs are finite; a program needn't handle non-finite values.
Results may differ from the reference program's by a relative error of at most 0.0004.
Values may be sent and summed in bfloat16 or wider, within the bound.
No kernel may reach another device: no remote copies, remote signals or barrier semaphores. Data moves between devices by JAX's collectives and lax.ppermute only.
A program may use at most 64 MiB of HBM per device.

```python
import math
import jax
import jax.numpy as jnp
from jax import lax

F = 1024
K = 128
PG = 4
HORIZON = 1024
PATHS = 8
N_PATHS = 2


def draw_log_persistence(key, part):
    key_pick, key_slow, key_fast = jax.random.split(key, 3)
    share = 0.5
    slow_mask = jax.random.uniform(key_pick, (F,), jnp.float32) < share
    slow_low = math.log(min(0.05 / HORIZON, 0.5 / 30.0))
    slow_high = math.log(min(2.0 / HORIZON, 1.0 / 30.0))
    slow_rate = jnp.exp(jax.random.uniform(key_slow, (F,), jnp.float32, slow_low, slow_high))
    fast_rate = jnp.exp(jax.random.uniform(key_fast, (F,), jnp.float32, math.log(1.0 / 50.0), math.log(1.0 / 30.0)))
    return -jnp.where(slow_mask, slow_rate, fast_rate)


def draw_regime_multiplier(key, part):
    key_day, key_size = jax.random.split(key)
    days = jax.random.randint(key_day, (4,), 0, HORIZON)
    sizes = jax.random.uniform(key_size, (4,), jnp.float32, 0.5, 0.8)
    return jnp.ones((HORIZON,), jnp.float32).at[days].set(sizes)


def steps_of(key, shape, cuts, smallest, largest):
    level, own = 1.0, jax.random.fold_in(key, 6)
    for position, shards_of in cuts:
        heights = jnp.exp(jax.random.uniform(jax.random.fold_in(own, position), (shards_of,), jnp.float32, smallest / len(cuts), largest / len(cuts)))
        level = level * jnp.repeat(heights, shape[position] // shards_of).reshape([-1 if axis == position else 1 for axis in range(len(shape))])
    return level


def gaussian(rng, extent, spread, limit, shards=(), held_as=jnp.bfloat16):
    level = steps_of(rng, extent, shards, -0.22, 0.18) if shards else 1.0
    drawn = jax.random.normal(rng, extent, jnp.float32) * spread * level
    return jnp.minimum(jnp.maximum(drawn, -limit), limit).astype(held_as)


def setup_inputs(seed: int = 0) -> dict:
    key_of = jax.random.split(jax.random.key(seed), 8)
    return {
        "independent_disturbances": gaussian(key_of[0], (HORIZON, PATHS, F), 1.0, 6.0, ((0, 16), (1, 2))),
        "starting_driver_values": gaussian(key_of[1], (PATHS, F), 1.0, 6.0, ((0, 2),), jnp.float32),
        "correlation_mixer": gaussian(key_of[2], (F, F), F ** -0.5, 0.1875, ((0, 2),)),
        "log_persistence": draw_log_persistence(jax.random.fold_in(key_of[7], 71), 0),
        "regime_multiplier": draw_regime_multiplier(jax.random.fold_in(key_of[7], 71), 0),
        "payoff_per_unit_table": gaussian(key_of[5], (F, K), F ** -0.5, 0.1875),
        "short_yield_coefficients": gaussian(key_of[6], (F,), F ** -0.5, 0.1875),
    }


def reference(independent_disturbances, starting_driver_values, correlation_mixer, log_persistence, regime_multiplier, payoff_per_unit_table, short_yield_coefficients):
    persistence_multiplier = jnp.exp(log_persistence)
    vol = jnp.sqrt(-jnp.expm1(2.0 * log_persistence))

    def one_group(group):
        start = (group * PG).astype(jnp.int32)
        block = lax.dynamic_slice_in_dim(independent_disturbances, start, PG, 1)
        leading_element = lax.dynamic_slice_in_dim(starting_driver_values, start, PG, 0)
        correlated_disturbances = jnp.dot(block.reshape(-1, F), correlation_mixer, preferred_element_type=jnp.float32).reshape(HORIZON, PG, F)

        def propagate_one_day(state, operand_tensors):
            random_normal_sample, driver_value_now = operand_tensors
            state = persistence_multiplier * driver_value_now * state + vol * random_normal_sample
            return (state, state)
        ignored_placeholder, driver_trajectory = lax.scan(propagate_one_day, leading_element, (correlated_disturbances, regime_multiplier))
        scenario = driver_trajectory.astype(jnp.bfloat16).reshape(-1, F)
        cash = jnp.dot(scenario, payoff_per_unit_table, preferred_element_type=jnp.float32).reshape(HORIZON, PG, K)
        rate = 0.03 + 0.3 * jnp.dot(scenario, short_yield_coefficients, preferred_element_type=jnp.float32).reshape(HORIZON, PG)
        discount = jnp.exp(-(1.0 / 256.0) * jnp.cumsum(rate, axis=0))
        return lax.optimization_barrier(jnp.sum(discount[:, :, None] * cash, axis=0)) / HORIZON
    result = lax.map(one_group, jnp.arange(N_PATHS, dtype=jnp.int32))
    return result.reshape(PATHS, K)
```

```python
import jax
import jax.numpy as jnp
from jax import lax
from jax.experimental import pallas as pl
from jax.experimental.pallas import tpu as pltpu
from jax.sharding import PartitionSpec as P

VMEM_BYTES = 16 * 1024 * 1024
LANES = 128


def exchange(a, axis, size, mask):
    return lax.ppermute(a, axis, perm=[(i, i ^ mask) for i in range(size)])


def in_vmem(count):
    return [pl.BlockSpec(memory_space=pltpu.VMEM)] * count


def call(body, out_shape, operands, scratch=(), flops=0):
    outs = jax.tree.leaves(out_shape)
    moved = sum(a.size * a.dtype.itemsize for a in [*operands, *outs])
    return pl.pallas_call(
        body,
        out_shape=out_shape,
        in_specs=in_vmem(len(operands)),
        out_specs=jax.tree.map(lambda _: in_vmem(1)[0], out_shape),
        scratch_shapes=scratch,
        compiler_params=pltpu.CompilerParams(vmem_limit_bytes=VMEM_BYTES),
        cost_estimate=pl.CostEstimate(flops=flops, bytes_accessed=moved, transcendentals=0),
    )(*operands)


def scan_body(chunks, paths, mixed_ref, left_ref, loading_ref, vol_ref, keep_ref, regime_ref, decay_ref, shock_ref, ends_ref, total_ref):
    steps, rows, factors = shock_ref.shape
    mixed = mixed_ref[...] + jnp.dot(left_ref[...], loading_ref[...], preferred_element_type=jnp.float32)
    shock_ref[...] = (mixed * vol_ref[...]).reshape(steps, rows, factors)
    keep = jnp.broadcast_to(keep_ref[...], (rows, factors))
    state = shock_ref[0]
    for i in range(1, steps):
        regime = jnp.concatenate([regime_ref[i]] * (factors // LANES), axis=1)
        state = (keep * regime) * state + shock_ref[i]
    ends_ref[...] = state
    total = state[:paths]
    for h in range(1, chunks):
        total = decay_ref[h : h + 1] * total + state[h * paths : (h + 1) * paths]
    total_ref[...] = total


def value_body(chunks, paths, sources, *refs):
    shock_ref, ends_ref, entering_ref = refs[:3]
    arrived = refs[3 : 3 + sources]
    weight_ref, keep_ref, regime_ref, decay_ref, table_ref, out_ref, scenario_ref = refs[3 + sources :]
    steps, rows, factors = shock_ref.shape
    instruments = table_ref.shape[1] - LANES
    first = entering_ref[...]
    for m in range(sources):
        first = first + weight_ref[m : m + 1] * arrived[m][...]
    starts = [first]
    for h in range(1, chunks):
        first = decay_ref[h - 1 : h] * first + ends_ref[(h - 1) * paths : h * paths]
        starts.append(first)
    state = jnp.concatenate(starts, axis=0) if chunks > 1 else first
    keep = jnp.broadcast_to(keep_ref[...], (rows, factors))
    held = []
    for i in range(steps):
        regime = jnp.concatenate([regime_ref[i]] * (factors // LANES), axis=1)
        state = (keep * regime) * state + shock_ref[i]
        held.append(state)
        if len(held) == 2 or i == steps - 1:
            block = jnp.concatenate(held, axis=0) if len(held) > 1 else held[0]
            scenario_ref[(i + 1) * rows - block.shape[0] : (i + 1) * rows] = block.astype(jnp.bfloat16)
            held = []
    both = jnp.dot(scenario_ref[...], table_ref[...], preferred_element_type=jnp.float32)
    running = jnp.zeros((rows, LANES), jnp.float32)
    sums = []
    for i in range(steps):
        running = running + (0.03 + 0.3 * both[i * rows : (i + 1) * rows, instruments:])
        sums.append(running)
    offsets, total = [], jnp.zeros((paths, LANES), jnp.float32)
    for h in range(chunks):
        offsets.append(total)
        total = total + running[h * paths : (h + 1) * paths]
    offset = jnp.concatenate(offsets, axis=0) if chunks > 1 else offsets[0]
    powers = [-(1.0 / 256.0) * (offset + s) for s in sums]
    peak = powers[0]
    for p in powers[1:]:
        peak = jnp.maximum(peak, p)
    top = peak[:paths]
    for h in range(1, chunks):
        top = jnp.maximum(top, peak[h * paths : (h + 1) * paths])
    peak = jnp.concatenate([top] * chunks, axis=0) if chunks > 1 else top
    valued = jnp.zeros((rows, instruments), jnp.float32)
    for i in range(steps):
        discount = jnp.exp(powers[i] - peak)
        wide = jnp.concatenate([discount] * (instruments // LANES), axis=1)
        valued = valued + wide * both[i * rows : (i + 1) * rows, :instruments]
    summed = valued[:paths]
    for h in range(1, chunks):
        summed = summed + valued[h * paths : (h + 1) * paths]
    lane = lax.broadcasted_iota(jnp.int32, (paths, LANES), 1)
    stats = jnp.where(lane < LANES // 2, total, top)
    stats = jnp.concatenate([stats] * (instruments // LANES), axis=1)
    out = jnp.concatenate([summed, stats], axis=0)
    for s in range(out_ref.shape[0]):
        out_ref[s] = out


def join_body(paths, days, parts_ref, out_ref):
    slabs, _, instruments = parts_ref.shape
    before = jnp.zeros((paths, instruments), jnp.float32)
    values = jnp.zeros((paths, instruments), jnp.float32)
    half = LANES // 2
    for s in range(slabs):
        part = parts_ref[s]
        total = jnp.broadcast_to(part[paths:, :1], (paths, instruments))
        top = jnp.broadcast_to(part[paths:, half : half + 1], (paths, instruments))
        values = values + jnp.exp(top - (1.0 / 256.0) * before) * part[:paths]
        before = before + total
    out_ref[...] = values * (1.0 / days)


def stages_of(size):
    bits = size.bit_length() - 1
    offset, stages = 0, []
    while offset < bits:
        width = min(2, bits - offset)
        stages.append((offset, 1 << width))
        offset += width
    return stages


def local(
    independent_disturbances,
    starting_driver_values,
    correlation_mixer,
    log_persistence,
    regime_multiplier,
    payoff_per_unit_table,
    short_yield_coefficients,
):
    days, paths, factors = independent_disturbances.shape
    instruments = payoff_per_unit_table.shape[1]
    rows_held = correlation_mixer.shape[0]
    groups, slabs = lax.axis_size("paths"), lax.axis_size("tm")
    group, place = lax.axis_index("paths"), lax.axis_index("tm")
    chunks = 8 // paths if paths < 8 and 8 % paths == 0 and days % (8 // paths) == 0 else 1
    steps, rows = days // chunks, chunks * paths
    f32 = jnp.float32

    core = place % 2
    pieces = 2
    cut = rows_held // (2 * pieces)
    received = []
    for k in range(1, groups):
        owner = (group - k) % groups
        for j in range(pieces):
            start = (core * pieces + j) * cut
            mine = lax.dynamic_slice_in_dim(correlation_mixer, start, cut, 0)
            got = lax.ppermute(mine, "paths", perm=[(i, (i + k) % groups) for i in range(groups)])
            received.append((owner * rows_held + start, got))
            other = exchange(got, "tm", slabs, 1)
            received.append((owner * rows_held + ((1 - core) * pieces + j) * cut, other))

    lanes = -(-slabs // LANES) * LANES
    lane = lax.broadcasted_iota(jnp.int32, (1, lanes), 1)
    regimes = jnp.where(lane == place, jnp.prod(regime_multiplier), 0.0)
    for b in range(slabs.bit_length() - 1):
        regimes = regimes + exchange(regimes, "tm", slabs, 1 << b)

    lows, highs, valid = [0 * place], [place], [place >= 0]
    stages = stages_of(slabs)

    def want(low, high, ok):
        lows.append(low)
        highs.append(high)
        valid.append(ok)
        return len(lows) - 1

    plan = []
    for offset, radix in stages:
        unit = 1 << offset
        base = place - place % (unit * radix)
        digit = (place // unit) % radix
        last = unit * radix == slabs
        whole = [None if last else want(base + ((digit ^ m) + 1) * unit, base + radix * unit, place >= 0) for m in range(radix)]
        ahead = [want(base + ((digit ^ m) + 1) * unit, place, (digit ^ m) < digit) for m in range(1, radix)]
        plan.append((unit, radix, whole, ahead))
    low, high, ok = jnp.stack(lows)[:, None], jnp.stack(highs)[:, None], jnp.stack(valid)[:, None]
    products = jnp.prod(jnp.where((lane >= low) & (lane < high), regimes, 1.0), axis=1, keepdims=True)
    spans = jnp.where(ok, (high - low) * days, 0).astype(f32)
    weights = jnp.where(ok, products * jnp.exp(spans * log_persistence[None, :]), 0.0)

    keep = jnp.exp(log_persistence)[None, :]
    vol = jnp.sqrt(-jnp.expm1(2.0 * log_persistence))[None, :]
    by_chunk = regime_multiplier.reshape(chunks, steps)
    decay = jnp.prod(by_chunk, axis=1)[:, None] * jnp.exp(float(steps) * log_persistence)[None, :]
    regime = jnp.broadcast_to(by_chunk.T[:, :, None, None], (steps, chunks, paths, LANES)).reshape(steps, rows, LANES)
    table = jnp.concatenate(
        [payoff_per_unit_table, jnp.broadcast_to(short_yield_coefficients[:, None], (factors, LANES))], axis=1
    )

    shocks = independent_disturbances.reshape(chunks, steps, paths, factors).transpose(1, 0, 2, 3).reshape(days * paths, factors)

    def columns(start, count):
        return lax.dynamic_slice_in_dim(shocks, start, count, 1)

    mixed = jnp.dot(columns(group * rows_held, rows_held), correlation_mixer, preferred_element_type=f32)
    for start, block in received[:-1]:
        mixed = mixed + jnp.dot(columns(start, cut), block, preferred_element_type=f32)
    start, block = received[-1]
    shock, ends, total = call(
        lambda *r: scan_body(chunks, paths, *r),
        (
            jax.ShapeDtypeStruct((steps, rows, factors), f32),
            jax.ShapeDtypeStruct((rows, factors), f32),
            jax.ShapeDtypeStruct((paths, factors), f32),
        ),
        (mixed, columns(start, cut), block, vol, keep, regime, decay),
        flops=2 * days * paths * cut * factors,
    )

    carried = weights[:1] * starting_driver_values
    for unit, radix, whole, ahead in plan:
        arrived = [exchange(total, "tm", slabs, m * unit) for m in range(1, radix)]
        if unit * radix < slabs:
            joined = weights[whole[0] : whole[0] + 1] * total
            for m, a in enumerate(arrived):
                joined = joined + weights[whole[m + 1] : whole[m + 1] + 1] * a
                carried = carried + weights[ahead[m] : ahead[m] + 1] * a
            total = joined

    parts = call(
        lambda *r: value_body(chunks, paths, len(arrived), *r),
        jax.ShapeDtypeStruct((slabs, 2 * paths, instruments), f32),
        (shock, ends, carried, *arrived, weights[ahead[0] : ahead[0] + len(ahead)], keep, regime, decay, table),
        scratch=[pltpu.VMEM((days * paths, factors), jnp.bfloat16)],
        flops=2 * days * paths * factors * (instruments + LANES),
    )
    gathered = lax.all_to_all(parts, "tm", 0, 0)
    return call(
        lambda *r: join_body(paths, days * slabs, *r),
        jax.ShapeDtypeStruct((paths, instruments), f32),
        (gathered,),
    )


def solution(mesh):
    in_specs = (P("tm", "paths", None), P("paths", None), P("paths", None), P(), P("tm"), P(), P())
    out_specs = P("paths", None)
    return jax.shard_map(local, mesh=mesh, in_specs=in_specs, out_specs=out_specs, check_vma=False)
```
